32 devices in a mesh: pipe: 4 (over x, core), dp: 2 (over y), mp: 4 (over z).
Axes of the slice: x: 2, y: 2, z: 4, core: 2. Of those that a mesh axis runs over, the one named last changes fastest.
Arguments:
- queries: bfloat16 [4, 4, 256, 8192], P('pipe', None, 'dp', 'mp'), may hold values from -6 to 6
- grad_out: bfloat16 [4, 4, 256, 8192], P('pipe', None, 'dp', 'mp'), may hold values from -6 to 6
- features: bfloat16 [4, 256, 8192], P('pipe', 'dp', 'mp'), may hold values from -6 to 6
- w_key: bfloat16 [4, 8192, 1024], P('pipe', ('mp', 'dp')), may hold values from -0.0625 to 0.0625
- w_value: bfloat16 [4, 8192, 1024], P('pipe', ('mp', 'dp')), may hold values from -0.0625 to 0.0625
- q_gain: float32 [4, 128], P('pipe'), may hold values from 0.1 to 1.9
- k_gain: float32 [4, 128], P('pipe'), may hold values from 0.1 to 1.9
- tile_counts: int32 [4, 2, 2], P(None, 'dp'), may hold values from 1 to 4, as said below
- image_starts: int32 [4, 2, 2], P(None, 'dp'), may hold values from 0 to 127, as said below
Outputs:
- feature_grads: bfloat16 [4, 256, 8192], P('pipe', 'dp', 'mp')
- key_weight_grads: bfloat16 [4, 8192, 1024], P('pipe', ('mp', 'dp'))
- value_weight_grads: bfloat16 [4, 8192, 1024], P('pipe', ('mp', 'dp'))
The draws below stay inside these ranges and needn't reach their ends.
Inputs may be any that keep to these rules, and one draw needn't show every extreme that they name: `tile_counts`: every image has at least one tile, and some image of some bin has 4 tiles. `image_starts`: within a bin the images' positions never fall.
All inputs are finite; a program needn't handle non-finite values.
Results may differ from the reference program's by a relative error of at most 0.028.
Values may be sent and summed in bfloat16 or wider, within the bound.
No kernel may reach another device: no remote copies, remote signals or barrier semaphores. Data moves between devices by JAX's collectives and lax.ppermute only.
A program may use at most 128 MiB of HBM per device.

```python
import math
import jax
import jax.numpy as jnp
from jax import lax

D = 8192
HD = 128
TOK = 128
TILE_TOK = 16
NIMG = 2
MAX_TILES = 4
M = 4
SECTIONS = 4
QW = 8192
KVW = 1024
TOKENS = 256
IMAGES = 256
N_DP = 2


def draw_tile_counts(key, part):
    values = jax.random.randint(key, (M, N_DP, NIMG), 1, MAX_TILES + 1, dtype=jnp.int32)
    return values.at[0, 0, 0].set(MAX_TILES)


def draw_image_starts(key, part):
    lead_key = jax.random.fold_in(key, 11)
    step_key = jax.random.fold_in(key, 23)
    leading = jax.random.randint(lead_key, (M, N_DP, 1), 0, TOK // 2, dtype=jnp.int32)
    increments = jax.random.randint(step_key, (M, N_DP, NIMG - 1), 0, TOK // 2, dtype=jnp.int32)
    return jnp.concatenate([leading, leading + jnp.cumsum(increments, axis=-1)], axis=-1)


def with_spikes(values, key, source, target, parts, factor):
    def block_of(axis_at):
        return (jnp.arange(values.shape[axis_at]) // (values.shape[axis_at] // parts)).reshape((-1,) + (1,) * (values.ndim - 1 - axis_at))

    near = jax.random.permutation(key, parts)[block_of(target)]
    second = (block_of(target) + parts // 2) % parts
    return jnp.where((block_of(source) == near) | (block_of(source) == second), factor * values, values)


def block_scale(own_key, dims, shards, low, top_value):
    def one(position, parts):
        steps = jax.random.uniform(jax.random.fold_in(jax.random.fold_in(own_key, 6), position), (parts,), jnp.float32, low / len(shards), top_value / len(shards))
        return jnp.repeat(jnp.exp(steps), dims[position] // parts).reshape((-1,) + (1,) * (len(dims) - position - 1))

    level = one(*shards[0])
    for cut in shards[1:]:
        level = level * one(*cut)
    return level


def centred(own_key, shape, width, limit, cuts=(), held_as=jnp.bfloat16):
    level = block_scale(own_key, shape, cuts, -0.22, 0.18) if cuts else 1.0
    values = jax.random.normal(own_key, shape, jnp.float32) * width * level
    return jnp.minimum(jnp.maximum(values, -limit), limit).astype(held_as)


def heavy_noise(own_key, shape, scale, limit, pieces, heavy, kind=jnp.bfloat16):
    result = scale * jax.random.normal(own_key, shape, jnp.float32)
    if pieces:
        result = result * block_scale(own_key, shape, pieces, -0.22, 0.18)
    return jnp.clip(with_spikes(result, jax.random.fold_in(own_key, 3), *heavy), -limit, limit).astype(kind)


def setup_inputs(seed: int = 0) -> dict:
    splits = jax.random.split(jax.random.key(seed), 10)
    queries = centred(splits[0], (SECTIONS, M, TOKENS, QW), 1.0, 6.0, ((0, 4), (2, 2), (3, 4)))
    grad_out = centred(splits[1], (SECTIONS, M, TOKENS, QW), 1.0, 6.0, ((0, 4), (2, 2), (3, 4)))
    features = heavy_noise(splits[2], (M, IMAGES, D), 1.0, 6.0, ((0, 4), (1, 2), (2, 4)), (1, 2, 4, 2.0))
    w_key = centred(splits[3], (SECTIONS, D, KVW), D ** -0.5, 0.0625, ((0, 4), (1, 8)))
    w_value = centred(splits[4], (SECTIONS, D, KVW), D ** -0.5, 0.0625, ((0, 4), (1, 8)))
    q_gain = jnp.clip(1.0 + 0.18 * jax.random.normal(splits[5], (SECTIONS, HD), jnp.float32), 0.1, 1.9)
    k_gain = jnp.clip(1.0 + 0.18 * jax.random.normal(splits[6], (SECTIONS, HD), jnp.float32), 0.1, 1.9)
    tile_counts = draw_tile_counts(jax.random.fold_in(splits[9], 71), 0)
    image_starts = draw_image_starts(jax.random.fold_in(splits[9], 71), 0)
    return {"queries": queries, "grad_out": grad_out, "features": features, "w_key": w_key, "w_value": w_value, "q_gain": q_gain, "k_gain": k_gain, "tile_counts": tile_counts, "image_starts": image_starts}


EPSILON = 1e-05

def normed(values, gain):
    inverse = lax.rsqrt(lax.optimization_barrier(jnp.mean(values * values, axis=-1, keepdims=True)) + EPSILON)
    return values * inverse * gain

def visible_slots(tile_counts, image_starts, image_len, text_len):
    lengths = tile_counts * TILE_TOK
    image_upper = jnp.cumsum(lengths, axis=-1)
    image_lower = image_upper - lengths
    slot_index = jnp.arange(image_len, dtype=jnp.int32)
    text_index = jnp.arange(text_len, dtype=jnp.int32)
    inside = ((slot_index >= image_lower[..., None]) & (slot_index < image_upper[..., None])).astype(jnp.float32)
    text_after = (text_index >= image_starts[..., None]).astype(jnp.float32)
    return jnp.einsum('...ij,...it->...jt', inside, text_after)

def attention_grads(query, grad_out, key_pre, value_rounded, visible, q_gain, k_gain):
    root_scale = 1.0 / math.sqrt(query.shape[-1])
    query_normed = normed(query.astype(jnp.float32), q_gain).astype(jnp.bfloat16)
    key_normed = normed(key_pre, k_gain).astype(jnp.bfloat16)
    scores = jnp.einsum('bjgd,btghd->bghjt', key_normed.astype(jnp.float32), query_normed.astype(jnp.float32)) * root_scale
    weights = jnp.exp(scores) * visible[:, None, None]
    denominator = lax.optimization_barrier(jnp.sum(weights, axis=3, keepdims=True))
    probability = weights / jnp.where(denominator > 0, denominator, 1.0)
    prob_rounded = probability.astype(jnp.bfloat16)
    value_grad = jnp.einsum('bghjt,btghd->bjgd', prob_rounded.astype(jnp.float32), grad_out.astype(jnp.float32)).astype(jnp.bfloat16)
    prob_grad = jnp.einsum('btghd,bjgd->bghjt', grad_out.astype(jnp.float32), value_rounded.astype(jnp.float32))
    row_delta = lax.optimization_barrier(jnp.sum(probability * prob_grad, axis=3, keepdims=True))
    score_grad = (probability * (prob_grad - row_delta)).astype(jnp.bfloat16)
    normed_grad = jnp.einsum('bghjt,btghd->bjgd', score_grad.astype(jnp.float32), query_normed.astype(jnp.float32)) * root_scale
    inverse = lax.rsqrt(lax.optimization_barrier(jnp.mean(key_pre * key_pre, axis=-1, keepdims=True)) + EPSILON)
    scaled = normed_grad * k_gain
    key_grad = inverse * scaled - key_pre * inverse ** 3 * lax.optimization_barrier(jnp.mean(scaled * key_pre, axis=-1, keepdims=True))
    return (key_grad.astype(jnp.bfloat16), value_grad)

def reference(queries, grad_out, features, w_key, w_value, q_gain, k_gain, tile_counts, image_starts):
    micro_count, image_count, model_width = features.shape
    replica_count = tile_counts.shape[1]
    image_len = image_count // replica_count
    text_len = queries.shape[2] // replica_count
    key_width = w_key.shape[2]
    head_dim = q_gain.shape[1]
    key_heads = key_width // head_dim
    groups = queries.shape[3] // key_width
    visible = visible_slots(tile_counts, image_starts, image_len, text_len)
    shape_q = (replica_count, text_len, key_heads, groups, head_dim)
    shape_k = (replica_count, image_len, key_heads, head_dim)
    factor = 1.0 / (micro_count * replica_count)

    def one_section(image_total, inputs):
        query_section, grad_section, key_weight, value_weight, query_gain, key_gain = inputs

        def one_batch(batch):
            feature_bin, query_bin, grad_bin, visible_bin = batch
            key_pre = jnp.dot(feature_bin, key_weight, preferred_element_type=jnp.float32)
            value_rounded = jnp.dot(feature_bin, value_weight, preferred_element_type=jnp.float32).astype(jnp.bfloat16)
            key_grad, value_grad = attention_grads(query_bin.reshape(shape_q), grad_bin.reshape(shape_q), key_pre.reshape(shape_k), value_rounded.reshape(shape_k), visible_bin, query_gain, key_gain)
            key_grad = key_grad.reshape(image_count, key_width)
            value_grad = value_grad.reshape(image_count, key_width)
            projected = jnp.dot(key_grad, key_weight.T, preferred_element_type=jnp.float32) + jnp.dot(value_grad, value_weight.T, preferred_element_type=jnp.float32)
            return (key_grad, value_grad, projected)
        key_grads, value_grads, projected = lax.map(one_batch, (features, query_section, grad_section, visible))

        def replica_term(totals, replica):
            start = (replica * image_len).astype(jnp.int32)
            feature_rows = lax.dynamic_slice_in_dim(features, start, image_len, 1).reshape(micro_count * image_len, model_width)
            key_rows = lax.dynamic_slice_in_dim(key_grads, start, image_len, 1).reshape(micro_count * image_len, key_width)
            value_rows = lax.dynamic_slice_in_dim(value_grads, start, image_len, 1).reshape(micro_count * image_len, key_width)
            key_term = jnp.dot(feature_rows.T, key_rows, preferred_element_type=jnp.float32).astype(jnp.bfloat16)
            value_term = jnp.dot(feature_rows.T, value_rows, preferred_element_type=jnp.float32).astype(jnp.bfloat16)
            key_term, value_term = lax.optimization_barrier((key_term, value_term))
            return ((totals[0] + key_term.astype(jnp.float32), totals[1] + value_term.astype(jnp.float32)), None)
        zeros = jnp.zeros((model_width, key_width), jnp.float32)
        totals, unused = lax.scan(replica_term, (zeros, zeros), jnp.arange(replica_count, dtype=jnp.int32))
        key_out = (totals[0] * factor).astype(jnp.bfloat16)
        value_out = (totals[1] * factor).astype(jnp.bfloat16)
        return (image_total + projected, (key_out, value_out))
    image_total, outs_pair = lax.scan(one_section, jnp.zeros(features.shape, jnp.float32), (queries, grad_out, w_key, w_value, q_gain, k_gain))
    return (image_total.astype(jnp.bfloat16), outs_pair[0], outs_pair[1])
```

```python
import functools
import math

import jax
import jax.numpy as jnp
from jax import lax
from jax.experimental import pallas as pl
from jax.experimental.pallas import tpu as pltpu
from jax.sharding import PartitionSpec as P

TILE_TOK = 16


EPSILON = 1e-05
ORDER = (0, 2, 1, 3)
SEQUENCE = (1, 2, 3, 0)

F32 = jnp.float32
BF16 = jnp.bfloat16


def dot_nt(a, b):
    return lax.dot_general(a, b, (((1,), (1,)), ((), ())), preferred_element_type=F32)


def dot_nn(a, b):
    return lax.dot_general(a, b, (((1,), (0,)), ((), ())), preferred_element_type=F32)


def cost(flops, moved, exps=0):
    return pl.CostEstimate(flops=flops, bytes_accessed=moved, transcendentals=exps)


def swap(values, axis, distance):
    size = lax.axis_size(axis)
    return lax.ppermute(values, axis, [(i, i ^ distance) for i in range(size)])


def query_norm_kernel(head_dim, q_ref, gain_ref, out_ref):
    gain = gain_ref[...]
    for start in range(0, q_ref.shape[2], head_dim):
        head = q_ref[0, :, start : start + head_dim].astype(F32)
        inverse = lax.rsqrt(jnp.mean(head * head, axis=-1, keepdims=True) + EPSILON)
        out_ref[0, :, start : start + head_dim] = (head * inverse * gain).astype(BF16)


def query_norm(query, gain):
    micro_count, text_len, width = query.shape
    block = pl.BlockSpec((1, text_len, width), lambda m: (m, 0, 0))
    return pl.pallas_call(
        functools.partial(query_norm_kernel, gain.shape[1]),
        out_shape=jax.ShapeDtypeStruct(query.shape, BF16),
        grid=(micro_count,),
        in_specs=[block, pl.BlockSpec(gain.shape, lambda m: (0, 0))],
        out_specs=block,
        cost_estimate=cost(6 * query.size, 4 * query.size),
        name="query_norm",
    )(query, gain)


def project_kernel(order_ref, own_ref, other_ref, wk_ref, wv_ref, keep_ref, send_ref):
    rows = own_ref.shape[0]
    part = wk_ref.shape[1]
    slots = jnp.concatenate([own_ref[...], other_ref[...]], axis=0)
    for at, weight in ((0, wk_ref), (part, wv_ref)):
        out = dot_nn(slots, weight[...])
        keep_ref[0, :, at : at + part] = out[:rows]
        send_ref[0, :, at : at + part] = out[rows:].astype(BF16)


def project(order, own, other, w_key, w_value):
    rows, depth = own.shape
    count = order.shape[0]
    part = w_key.shape[1] // count
    whole = pl.BlockSpec((rows, depth), lambda c, o: (0, 0))
    weight = pl.BlockSpec((depth, part), lambda c, o: (0, o[c]))
    out = pl.BlockSpec((1, rows, 2 * part), lambda c, o: (c, 0, 0))
    shape = (count, rows, 2 * part)
    return pl.pallas_call(
        project_kernel,
        out_shape=(jax.ShapeDtypeStruct(shape, F32), jax.ShapeDtypeStruct(shape, BF16)),
        grid_spec=pltpu.PrefetchScalarGridSpec(
            num_scalar_prefetch=1,
            grid=(count,),
            in_specs=[whole, whole, weight, weight],
            out_specs=[out, out],
        ),
        cost_estimate=cost(
            8 * rows * depth * part * count, 4 * depth * part * count + 12 * rows * part * count
        ),
        name="project",
    )(order, own, other, w_key, w_value)


def attention_kernel(
    head_dim,
    image_count,
    micro_ref,
    tiles_ref,
    starts_ref,
    q_ref,
    go_ref,
    keep_ref,
    first_ref,
    second_ref,
    third_ref,
    gain_ref,
    out_ref,
):
    micro = micro_ref[0]
    summed = (
        keep_ref[0]
        + first_ref[0].astype(F32)
        + second_ref[0].astype(F32)
        + third_ref[...].astype(F32)
    )
    image_len, width = summed.shape
    local_width = width // 2
    key_heads = local_width // head_dim
    text_len = q_ref.shape[1]
    groups = q_ref.shape[2] // local_width
    gain = gain_ref[...]
    root_scale = 1.0 / math.sqrt(head_dim)
    slot = lax.broadcasted_iota(jnp.int32, (image_len, text_len), 0)
    text = lax.broadcasted_iota(jnp.int32, (image_len, text_len), 1)
    seen = jnp.zeros((image_len, text_len), F32)
    lower = jnp.int32(0)
    for image in range(image_count):
        upper = lower + tiles_ref[micro * image_count + image] * TILE_TOK
        begin = starts_ref[micro * image_count + image]
        inside = (slot >= lower) & (slot < upper) & (text >= begin)
        seen = jnp.where(inside, 1.0, seen)
        lower = upper
    seen = jnp.concatenate([seen] * groups, axis=1)
    for g in range(key_heads):
        key_pre = summed[:, g * head_dim : (g + 1) * head_dim]
        value = summed[:, local_width + g * head_dim : local_width + (g + 1) * head_dim]
        value = value.astype(BF16)
        inverse = lax.rsqrt(jnp.mean(key_pre * key_pre, axis=-1, keepdims=True) + EPSILON)
        key = (key_pre * inverse * gain).astype(BF16)
        heads = [(g * groups + h) * head_dim for h in range(groups)]
        query = jnp.concatenate([q_ref[0, :, h : h + head_dim] for h in heads], axis=0)
        grad = jnp.concatenate([go_ref[0, :, h : h + head_dim] for h in heads], axis=0)
        weights = jnp.exp(dot_nt(key, query) * root_scale) * seen
        total = jnp.sum(weights, axis=0, keepdims=True)
        probability = weights * (1.0 / jnp.where(total > 0, total, 1.0))
        value_grad = dot_nn(probability.astype(BF16), grad)
        prob_grad = dot_nt(value, grad)
        delta = jnp.sum(probability * prob_grad, axis=0, keepdims=True)
        score_grad = (probability * (prob_grad - delta)).astype(BF16)
        scaled = dot_nn(score_grad, query) * root_scale * gain
        key_grad = inverse * scaled - key_pre * inverse**3 * jnp.mean(
            scaled * key_pre, axis=-1, keepdims=True
        )
        out_ref[:, g * head_dim : (g + 1) * head_dim] = key_grad.astype(BF16)
        at = local_width + g * head_dim
        out_ref[:, at : at + head_dim] = value_grad.astype(BF16)


def attention(micro, tiles, starts, query, grad_out, keep, first, second, third, gain):
    image_len, width = third.shape
    _, text_len, query_width = query.shape
    image_count = tiles.shape[0] // query.shape[0]
    head_dim = gain.shape[1]
    texts = pl.BlockSpec((1, text_len, query_width), lambda i, m, t, s: (m[0], 0, 0))
    block = pl.BlockSpec((1, image_len, width), lambda i, m, t, s: (0, 0, 0))
    plain = pl.BlockSpec((image_len, width), lambda i, m, t, s: (0, 0))
    return pl.pallas_call(
        functools.partial(attention_kernel, head_dim, image_count),
        out_shape=jax.ShapeDtypeStruct((image_len, width), BF16),
        grid_spec=pltpu.PrefetchScalarGridSpec(
            num_scalar_prefetch=3,
            grid=(1,),
            in_specs=[
                texts,
                texts,
                block,
                block,
                block,
                plain,
                pl.BlockSpec(gain.shape, lambda i, m, t, s: (0, 0)),
            ],
            out_specs=plain,
        ),
        cost_estimate=cost(
            8 * image_len * text_len * query_width,
            4 * text_len * query_width + 12 * image_len * width,
            image_len * text_len * query_width // head_dim,
        ),
        name="attention",
    )(micro, tiles, starts, query, grad_out, keep, first, second, third, gain)


def feature_grad_kernel(order_ref, own_ref, other_ref, wk_ref, wv_ref, out_ref, total_ref):
    rows = own_ref.shape[1]
    part = wk_ref.shape[1]
    step = pl.program_id(0)
    grads = jnp.concatenate([own_ref[0], other_ref[0]], axis=0)
    term = dot_nt(grads[:, :part], wk_ref[...]) + dot_nt(grads[:, part:], wv_ref[...])

    @pl.when(step == 0)
    def _():
        total_ref[...] = term

    @pl.when(step > 0)
    def _():
        total_ref[...] += term

    @pl.when(step == pl.num_programs(0) - 1)
    def _():
        out_ref[0] = total_ref[:rows].astype(out_ref.dtype)
        out_ref[1] = total_ref[rows:].astype(out_ref.dtype)


def feature_grad(order, own, other, w_key, w_value, kind):
    count, rows, width = own.shape
    depth = w_key.shape[0]
    part = width // 2
    grads = pl.BlockSpec((1, rows, width), lambda c, o: (c, 0, 0))
    weight = pl.BlockSpec((depth, part), lambda c, o: (0, o[c]))
    return pl.pallas_call(
        feature_grad_kernel,
        out_shape=jax.ShapeDtypeStruct((2, rows, depth), kind),
        grid_spec=pltpu.PrefetchScalarGridSpec(
            num_scalar_prefetch=1,
            grid=(count,),
            in_specs=[grads, grads, weight, weight],
            out_specs=pl.BlockSpec((2, rows, depth), lambda c, o: (0, 0, 0)),
            scratch_shapes=[pltpu.VMEM((2 * rows, depth), F32)],
        ),
        cost_estimate=cost(
            8 * rows * depth * part * count, 4 * depth * part * count + 8 * rows * part * count
        ),
        name="feature_grad",
    )(order, own, other, w_key, w_value)


def weight_grad_kernel(pieces, factor, order_ref, *refs):
    slots = refs[:pieces]
    grads = refs[pieces : 2 * pieces]
    key_ref, value_ref, turned_ref = refs[2 * pieces :]
    rows = slots[0].shape[0]
    part = key_ref.shape[1]

    @pl.when(pl.program_id(0) == 0)
    def _():
        for n in range(pieces):
            turned_ref[:, n * rows : (n + 1) * rows] = slots[n][...].T

    every = jnp.concatenate([g[0] for g in grads], axis=0)
    turned = turned_ref[...]
    key_ref[...] = (dot_nn(turned, every[:, :part]) * factor).astype(BF16)
    value_ref[...] = (dot_nn(turned, every[:, part:]) * factor).astype(BF16)


def weight_grad(order, slots, grads, factor):
    rows, depth = slots[0].shape
    count, _, width = grads[0].shape
    part = width // 2
    pieces = len(slots)
    slot = pl.BlockSpec((rows, depth), lambda c, o: (0, 0))
    grad = pl.BlockSpec((1, rows, width), lambda c, o: (c, 0, 0))
    out = pl.BlockSpec((depth, part), lambda c, o: (0, o[c]))
    shape = jax.ShapeDtypeStruct((depth, part * count), BF16)
    return pl.pallas_call(
        functools.partial(weight_grad_kernel, pieces, factor),
        out_shape=(shape, shape),
        grid_spec=pltpu.PrefetchScalarGridSpec(
            num_scalar_prefetch=1,
            grid=(count,),
            in_specs=[slot] * pieces + [grad] * pieces,
            out_specs=[out, out],
            scratch_shapes=[pltpu.VMEM((depth, pieces * rows), BF16)],
        ),
        cost_estimate=cost(
            2 * pieces * rows * depth * width * count,
            2 * pieces * rows * (depth + width * count) + 2 * depth * width * count,
        ),
        name="weight_grad",
    )(order, *slots, *grads)


def per_device_pair(
    queries, grad_out, features, w_key, w_value, q_gain, k_gain, tile_counts, image_starts
):
    own_pipe = lax.axis_index("pipe")
    own_dp = lax.axis_index("dp")
    own_mp = lax.axis_index("mp")
    micro_count = queries.shape[1]
    order = jnp.stack([own_mp ^ c for c in ORDER]).astype(jnp.int32)
    tiles = tile_counts.reshape(-1)
    starts = image_starts.reshape(-1)
    w_key = w_key[0]
    w_value = w_value[0]
    half = w_key.shape[0]
    local = features[0]
    image_len = local.shape[0]

    mine = lax.dynamic_slice(local, (0, own_dp * half), (image_len, half))
    theirs = lax.dynamic_slice(local, (0, (1 - own_dp) * half), (image_len, half))
    slots = {0: jnp.stack([mine, swap(theirs, "dp", 1)])}
    slots[1] = swap(slots[0], "pipe", 1)
    slots[2] = swap(slots[0], "pipe", 2)
    slots[3] = swap(slots[2], "pipe", 1)

    query = query_norm(queries[0], q_gain)

    grads = {}
    image = {}
    for j in SEQUENCE:
        keep, send = project(order, slots[j][0], slots[j][1], w_key, w_value)
        first = swap(send, "dp", 1)
        send = (keep[2:] + first[2:].astype(F32)).astype(BF16)
        second = swap(send, "mp", 1)
        send = (keep[1] + first[1].astype(F32) + second[1].astype(F32)).astype(BF16)
        third = swap(send, "mp", 2)
        micro = (own_pipe ^ j).astype(jnp.int32).reshape(1)
        grad = attention(
            micro, tiles, starts, query, grad_out[0], keep, first, second, third, k_gain
        )
        far = swap(grad, "mp", 2)
        pair = jnp.stack([grad, far])
        near = swap(pair, "mp", 1)
        own = jnp.concatenate([pair, near], axis=0)
        grads[j] = (own, swap(own, "dp", 1))
    for j in SEQUENCE:
        own, other = grads[j]
        if j:
            image[j] = swap(
                feature_grad(order, own, other, w_key, w_value, BF16), "pipe", j
            ).astype(F32)
        else:
            image[j] = feature_grad(order, own, other, w_key, w_value, F32)
    total = image[0] + image[1] + image[2] + image[3]
    other_half = swap(total[1].astype(BF16), "dp", 1)
    own_half = total[0].astype(BF16)
    image_grads = jnp.where(
        own_dp == 0,
        jnp.concatenate([own_half, other_half], axis=1),
        jnp.concatenate([other_half, own_half], axis=1),
    )
    factor = 1.0 / (micro_count * 2)
    key_out, value_out = weight_grad(
        order,
        [slots[j][r] for j in range(micro_count) for r in range(2)],
        [grads[j][r] for j in range(micro_count) for r in range(2)],
        factor,
    )
    return image_grads[None], key_out[None], value_out[None]


def normed(values, gain):
    inverse = lax.rsqrt(jnp.mean(values * values, axis=-1, keepdims=True) + EPSILON)
    return values * inverse * gain


def visible_slots(tile_counts, image_starts, image_len, text_len):
    lengths = tile_counts * TILE_TOK
    image_upper = jnp.cumsum(lengths, axis=-1)
    image_lower = image_upper - lengths
    slot_index = jnp.arange(image_len, dtype=jnp.int32)
    text_index = jnp.arange(text_len, dtype=jnp.int32)
    inside = (
        (slot_index >= image_lower[..., None]) & (slot_index < image_upper[..., None])
    ).astype(jnp.float32)
    text_after = (text_index >= image_starts[..., None]).astype(jnp.float32)
    return jnp.einsum("...ij,...it->...jt", inside, text_after)


def attention_grads(query, grad_out, key_pre, value_rounded, visible, q_gain, k_gain):
    root_scale = 1.0 / math.sqrt(query.shape[-1])
    query_normed = normed(query.astype(jnp.float32), q_gain).astype(jnp.bfloat16)
    key_normed = normed(key_pre, k_gain).astype(jnp.bfloat16)
    scores = (
        jnp.einsum(
            "bjgd,btghd->bghjt", key_normed, query_normed, preferred_element_type=jnp.float32
        )
        * root_scale
    )
    weights = jnp.exp(scores) * visible[:, None, None]
    denominator = jnp.sum(weights, axis=3, keepdims=True)
    probability = weights / jnp.where(denominator > 0, denominator, 1.0)
    prob_rounded = probability.astype(jnp.bfloat16)
    value_grad = jnp.einsum(
        "bghjt,btghd->bjgd", prob_rounded, grad_out, preferred_element_type=jnp.float32
    ).astype(jnp.bfloat16)
    prob_grad = jnp.einsum(
        "btghd,bjgd->bghjt", grad_out, value_rounded, preferred_element_type=jnp.float32
    )
    row_delta = jnp.sum(probability * prob_grad, axis=3, keepdims=True)
    score_grad = (probability * (prob_grad - row_delta)).astype(jnp.bfloat16)
    normed_grad = (
        jnp.einsum(
            "bghjt,btghd->bjgd", score_grad, query_normed, preferred_element_type=jnp.float32
        )
        * root_scale
    )
    inverse = lax.rsqrt(jnp.mean(key_pre * key_pre, axis=-1, keepdims=True) + EPSILON)
    scaled = normed_grad * k_gain
    key_grad = inverse * scaled - key_pre * inverse**3 * jnp.mean(
        scaled * key_pre, axis=-1, keepdims=True
    )
    return (key_grad.astype(jnp.bfloat16), value_grad)


def per_device(
    queries, grad_out, features, w_key, w_value, q_gain, k_gain, tile_counts, image_starts
):
    head_dim = q_gain.shape[1]
    features_all = lax.all_gather(features, "pipe", axis=0, tiled=True)
    micro_count, image_len, quarter = features_all.shape
    slot_rows = micro_count * image_len
    flattened = features_all.reshape(slot_rows, quarter)
    weight_pair = lax.all_gather(jnp.stack([w_key[0], w_value[0]]), "dp", axis=1, tiled=True)
    key_width = weight_pair.shape[2]
    partial_kv = jnp.einsum(
        "bi,sik->bsk", flattened, weight_pair, preferred_element_type=jnp.float32
    )
    summed_kv = lax.psum_scatter(
        partial_kv.astype(jnp.bfloat16), "mp", scatter_dimension=2, tiled=True
    ).astype(jnp.float32)
    local_width = summed_kv.shape[2]
    key_heads = local_width // head_dim
    query_local = queries[0]
    text_len = query_local.shape[1]
    groups = query_local.shape[2] // local_width
    shape_q = (micro_count, text_len, key_heads, groups, head_dim)
    shape_k = (micro_count, image_len, key_heads, head_dim)
    visible = visible_slots(tile_counts[:, 0], image_starts[:, 0], image_len, text_len)
    key_grad, value_grad = attention_grads(
        query_local.reshape(shape_q),
        grad_out[0].reshape(shape_q),
        summed_kv[:, 0].reshape(shape_k),
        summed_kv[:, 1].astype(jnp.bfloat16).reshape(shape_k),
        visible,
        q_gain[0],
        k_gain[0],
    )
    local_grads = jnp.stack(
        [key_grad.reshape(slot_rows, local_width), value_grad.reshape(slot_rows, local_width)],
        axis=1,
    )
    kv_grads = lax.all_gather(local_grads, "mp", axis=2, tiled=True)
    image_grads = lax.psum_scatter(
        jnp.einsum("bsk,sik->bi", kv_grads, weight_pair, preferred_element_type=jnp.float32).astype(
            jnp.bfloat16
        ),
        "pipe",
        scatter_dimension=0,
        tiled=True,
    ).astype(jnp.float32)
    dp_count = lax.axis_size("dp")
    factor = 1.0 / (micro_count * dp_count)
    columns = lax.all_to_all(flattened, "dp", split_axis=1, concat_axis=0, tiled=True)
    every_grad = lax.all_gather(kv_grads, "dp", axis=0, tiled=True)
    columns = columns.reshape(dp_count, slot_rows, quarter // dp_count)
    every_grad = every_grad.reshape(dp_count, slot_rows, 2, key_width)
    replica_terms = jnp.einsum(
        "rbi,rbsk->risk", columns, every_grad, preferred_element_type=jnp.float32
    ).astype(jnp.bfloat16)
    replica_terms = lax.optimization_barrier(replica_terms)
    summed = jnp.sum(replica_terms.astype(jnp.float32), axis=0)
    scaled_grads = (summed * factor).astype(jnp.bfloat16)
    return (
        image_grads.reshape(1, image_len, quarter).astype(jnp.bfloat16),
        scaled_grads[:, 0][None],
        scaled_grads[:, 1][None],
    )


def solution(mesh):
    in_specs = (
        P("pipe", None, "dp", "mp"),
        P("pipe", None, "dp", "mp"),
        P("pipe", "dp", "mp"),
        P("pipe", ("mp", "dp"), None),
        P("pipe", ("mp", "dp"), None),
        P("pipe", None),
        P("pipe", None),
        P(None, "dp", None),
        P(None, "dp", None),
    )
    out_specs = (
        P("pipe", "dp", "mp"),
        P("pipe", ("mp", "dp"), None),
        P("pipe", ("mp", "dp"), None),
    )
    paired = (mesh.shape["pipe"], mesh.shape["dp"], mesh.shape["mp"]) == (4, 2, 4)
    return jax.shard_map(
        per_device_pair if paired else per_device,
        mesh=mesh,
        in_specs=in_specs,
        out_specs=out_specs,
        check_vma=False,
    )
```

```python
import functools
import math

import jax
import jax.numpy as jnp
from jax import lax
from jax.experimental import pallas as pl
from jax.experimental.pallas import tpu as pltpu
from jax.sharding import PartitionSpec as P

TILE_TOK = 16


EPSILON = 1e-05
ORDER = (0, 2, 1, 3)
SEQUENCE = (1, 2, 3, 0)

F32 = jnp.float32
BF16 = jnp.bfloat16
MIB = 1024 * 1024


def dot_nt(a, b):
    return lax.dot_general(a, b, (((1,), (1,)), ((), ())), preferred_element_type=F32)


def dot_nn(a, b):
    return lax.dot_general(a, b, (((1,), (0,)), ((), ())), preferred_element_type=F32)


def swap(values, axis, distance):
    size = lax.axis_size(axis)
    return lax.ppermute(values, axis, [(i, i ^ distance) for i in range(size)])


class Line:
    def __init__(self):
        self.last = None

    def __call__(self, body, outs, scalars, arrays, flops=0, grid=(), out_specs=None, limit=16):
        vmem = pl.BlockSpec(memory_space=pltpu.VMEM)
        smem = pl.BlockSpec(memory_space=pltpu.SMEM)
        after = [] if self.last is None else [self.last]
        inputs = len(scalars) + len(arrays)

        def kernel(*refs):
            body(*refs[:inputs], *refs[inputs + len(after) :])

        moved = sum(2 * a.size for a in arrays)
        results = pl.pallas_call(
            kernel,
            out_shape=outs,
            grid=grid,
            in_specs=[smem] * len(scalars)
            + [vmem] * len(arrays)
            + [pl.BlockSpec(memory_space=pl.ANY)] * len(after),
            out_specs=out_specs if out_specs is not None else [vmem] * len(outs),
            cost_estimate=pl.CostEstimate(flops=flops, bytes_accessed=moved, transcendentals=0),
            compiler_params=pltpu.CompilerParams(vmem_limit_bytes=limit * MIB),
            name=body.__name__ if hasattr(body, "__name__") else body.func.__name__,
        )(*scalars, *arrays, *after)
        self.last = results[-1]
        return results


def shape(*dims, kind=BF16):
    return jax.ShapeDtypeStruct(dims, kind)


def columns(order_ref, c, part):
    return pl.ds(pl.multiple_of(order_ref[c] * part, part), part)


def query_norm(q_ref, gain_ref, out_ref):
    gain = gain_ref[...]
    head_dim = gain.shape[1]
    for micro in range(q_ref.shape[0]):
        for start in range(0, q_ref.shape[2], head_dim):
            head = q_ref[micro, :, start : start + head_dim].astype(F32)
            inverse = lax.rsqrt(jnp.mean(head * head, axis=-1, keepdims=True) + EPSILON)
            out_ref[micro, :, start : start + head_dim] = (head * inverse * gain).astype(BF16)


def turn(slots_ref, out_ref):
    rows = slots_ref.shape[1]
    for replica in range(slots_ref.shape[0]):
        out_ref[:, replica * rows : (replica + 1) * rows] = slots_ref[replica].T


def project(order_ref, slots_ref, wk_ref, wv_ref, keep_ref, send_ref):
    count, rows, width = keep_ref.shape
    part = width // 2
    slots = jnp.concatenate([slots_ref[0], slots_ref[1]], axis=0)
    for c in range(count):
        for at, weight in ((0, wk_ref), (part, wv_ref)):
            out = dot_nn(slots, weight[:, columns(order_ref, c, part)])
            keep_ref[c, :, at : at + part] = out[:rows]
            send_ref[c, :, at : at + part] = out[rows:].astype(BF16)


def add_first(keep_ref, first_ref, out_ref):
    out_ref[...] = (keep_ref[2:] + first_ref[2:].astype(F32)).astype(BF16)


def add_second(keep_ref, first_ref, second_ref, out_ref):
    out = keep_ref[1] + first_ref[1].astype(F32) + second_ref[1].astype(F32)
    out_ref[...] = out.astype(BF16)


def attention(
    micro_ref,
    tiles_ref,
    starts_ref,
    q_ref,
    go_ref,
    keep_ref,
    first_ref,
    second_ref,
    third_ref,
    gain_ref,
    out_ref,
):
    micro = micro_ref[0]
    gain = gain_ref[...]
    head_dim = gain.shape[1]
    summed = (
        keep_ref[0]
        + first_ref[0].astype(F32)
        + second_ref[0].astype(F32)
        + third_ref[...].astype(F32)
    )
    image_len, width = summed.shape
    local_width = width // 2
    key_heads = local_width // head_dim
    text_len = q_ref.shape[1]
    groups = q_ref.shape[2] // local_width
    root_scale = 1.0 / math.sqrt(head_dim)
    slot = lax.broadcasted_iota(jnp.int32, (image_len, text_len), 0)
    text = lax.broadcasted_iota(jnp.int32, (image_len, text_len), 1)
    seen = jnp.zeros((image_len, text_len), F32)
    lower = jnp.int32(0)
    for image in range(tiles_ref.shape[1]):
        upper = lower + tiles_ref[micro, image] * TILE_TOK
        inside = (slot >= lower) & (slot < upper) & (text >= starts_ref[micro, image])
        seen = jnp.where(inside, 1.0, seen)
        lower = upper
    seen = jnp.concatenate([seen] * groups, axis=1)
    for g in range(key_heads):
        key_pre = summed[:, g * head_dim : (g + 1) * head_dim]
        value = summed[:, local_width + g * head_dim : local_width + (g + 1) * head_dim]
        value = value.astype(BF16)
        inverse = lax.rsqrt(jnp.mean(key_pre * key_pre, axis=-1, keepdims=True) + EPSILON)
        key = (key_pre * inverse * gain).astype(BF16)
        heads = [(g * groups + h) * head_dim for h in range(groups)]
        query = jnp.concatenate([q_ref[micro, :, h : h + head_dim] for h in heads], axis=0)
        grad = jnp.concatenate([go_ref[micro, :, h : h + head_dim] for h in heads], axis=0)
        weights = jnp.exp(dot_nt(key, query) * root_scale) * seen
        total = jnp.sum(weights, axis=0, keepdims=True)
        probability = weights * (1.0 / jnp.where(total > 0, total, 1.0))
        value_grad = dot_nn(probability.astype(BF16), grad)
        prob_grad = dot_nt(value, grad)
        delta = jnp.sum(probability * prob_grad, axis=0, keepdims=True)
        score_grad = (probability * (prob_grad - delta)).astype(BF16)
        scaled = dot_nn(score_grad, query) * root_scale * gain
        key_grad = inverse * scaled - key_pre * inverse**3 * jnp.mean(
            scaled * key_pre, axis=-1, keepdims=True
        )
        out_ref[:, g * head_dim : (g + 1) * head_dim] = key_grad.astype(BF16)
        at = local_width + g * head_dim
        out_ref[:, at : at + head_dim] = value_grad.astype(BF16)


def join_far(own_ref, far_ref, out_ref):
    out_ref[0] = own_ref[...]
    out_ref[1] = far_ref[...]


def join_near(pair_ref, near_ref, out_ref):
    out_ref[:2] = pair_ref[...]
    out_ref[2:] = near_ref[...]


def feature_grad(order_ref, own_ref, other_ref, wk_ref, wv_ref, out_ref):
    count, rows, width = own_ref.shape
    part = width // 2
    depth = wk_ref.shape[0]
    tile = min(depth, 256)
    grads = jnp.concatenate(
        [jnp.concatenate([g[c] for c in range(count)], axis=1) for g in (own_ref, other_ref)],
        axis=0,
    )
    for start in range(0, depth, tile):
        weights = jnp.concatenate(
            [
                weight[start : start + tile, columns(order_ref, c, part)]
                for c in range(count)
                for weight in (wk_ref, wv_ref)
            ],
            axis=1,
        )
        out = dot_nt(grads, weights).astype(out_ref.dtype)
        out_ref[0, :, start : start + tile] = out[:rows]
        out_ref[1, :, start : start + tile] = out[rows:]


def weight_grad(pieces, factor, order_ref, *refs):
    turned = refs[:pieces]
    grads = refs[pieces : 3 * pieces]
    key_ref, value_ref = refs[3 * pieces :]
    part = key_ref.shape[1]
    step = pl.program_id(0)
    every = jnp.concatenate([g[step] for g in grads], axis=0)
    slots = jnp.concatenate([t[...] for t in turned], axis=1)
    key_ref[...] = (dot_nn(slots, every[:, :part]) * factor).astype(BF16)
    value_ref[...] = (dot_nn(slots, every[:, part:]) * factor).astype(BF16)


def per_device_pair(
    queries, grad_out, features, w_key, w_value, q_gain, k_gain, tile_counts, image_starts
):
    own_pipe = lax.axis_index("pipe")
    own_dp = lax.axis_index("dp")
    own_mp = lax.axis_index("mp")
    micro_count = queries.shape[1]
    order = jnp.stack([own_mp ^ c for c in ORDER]).astype(jnp.int32)
    micros = {j: (own_pipe ^ j).astype(jnp.int32).reshape(1) for j in SEQUENCE}
    tiles = tile_counts[:, 0]
    starts = image_starts[:, 0]
    w_key = w_key[0]
    w_value = w_value[0]
    half, key_width = w_key.shape
    local = features[0]
    image_len = local.shape[0]
    count = len(ORDER)
    width = 2 * key_width // count
    dense = 4 * 2 * image_len * half * key_width

    mine = lax.dynamic_slice(local, (0, own_dp * half), (image_len, half))
    theirs = lax.dynamic_slice(local, (0, (1 - own_dp) * half), (image_len, half))
    slots = {0: jnp.stack([mine, swap(theirs, "dp", 1)])}
    slots[1] = swap(slots[0], "pipe", 1)
    slots[2] = swap(slots[0], "pipe", 2)
    slots[3] = swap(slots[2], "pipe", 1)

    line = Line()
    keep, first, second, third = {}, {}, {}, {}
    grad, pair, near, own, other, image, turned = {}, {}, {}, {}, {}, {}, {}

    def run_project(j):
        keep[j], send = line(
            project,
            [shape(count, image_len, width, kind=F32), shape(count, image_len, width)],
            [order],
            [slots[j], w_key, w_value],
            dense,
        )
        first[j] = swap(send, "dp", 1)

    def run_turn(j):
        (turned[j],) = line(turn, [shape(half, 2 * image_len)], [], [slots[j]])

    def run_first(j):
        (send,) = line(add_first, [shape(2, image_len, width)], [], [keep[j], first[j]])
        second[j] = swap(send, "mp", 1)

    def run_second(j):
        (send,) = line(
            add_second, [shape(image_len, width)], [], [keep[j], first[j], second[j]]
        )
        third[j] = swap(send, "mp", 2)

    def run_attention(j):
        (grad[j],) = line(
            attention,
            [shape(image_len, width)],
            [micros[j], tiles, starts],
            [query, grad_out[0], keep[j], first[j], second[j], third[j], k_gain],
            dense // 2,
        )
        pair[j] = swap(grad[j], "mp", 2)

    def run_far(j):
        (pair[j],) = line(join_far, [shape(2, image_len, width)], [], [grad[j], pair[j]])
        near[j] = swap(pair[j], "mp", 1)

    def run_near(j):
        (own[j],) = line(join_near, [shape(count, image_len, width)], [], [pair[j], near[j]])
        other[j] = swap(own[j], "dp", 1)

    def run_image(j):
        (out,) = line(
            feature_grad,
            [shape(2, image_len, half, kind=BF16 if j else F32)],
            [order],
            [own[j], other[j], w_key, w_value],
            dense,
        )
        image[j] = swap(out, "pipe", j).astype(F32) if j else out

    a, b, c, d = SEQUENCE
    run_project(a)
    (query,) = line(query_norm, [shape(*queries.shape[1:])], [], [queries[0], q_gain])
    run_turn(a)
    run_project(b)
    run_turn(b)
    run_project(c)
    run_project(d)
    run_first(a)
    run_turn(c)
    run_second(a)
    run_first(b)
    run_turn(d)
    run_attention(a)
    run_second(b)
    run_first(c)
    run_attention(b)
    run_second(c)
    run_far(a)
    run_first(d)
    run_near(a)
    run_attention(c)
    run_second(d)
    run_far(b)
    run_near(b)
    run_attention(d)
    run_image(a)
    run_far(c)
    run_near(c)
    run_image(b)
    run_far(d)
    run_near(d)
    run_image(c)
    run_image(d)

    total = image[0] + image[1] + image[2] + image[3]
    other_half = swap(total[1].astype(BF16), "dp", 1)
    own_half = total[0].astype(BF16)
    image_grads = jnp.where(
        own_dp == 0,
        jnp.concatenate([own_half, other_half], axis=1),
        jnp.concatenate([other_half, own_half], axis=1),
    )
    factor = 1.0 / (micro_count * 2)
    key_out, value_out = weight_outputs(
        line, order, [turned[j] for j in SEQUENCE], [(own[j], other[j]) for j in SEQUENCE], factor
    )
    return image_grads[None], key_out[None], value_out[None]


def weight_outputs(line, order, turned, grads, factor):
    depth = turned[0].shape[0]
    count, _, width = grads[0][0].shape
    part = width // 2
    flat = [g for two in grads for g in two]
    vmem = pl.BlockSpec(memory_space=pltpu.VMEM)
    out = pl.BlockSpec((depth, part), lambda c, o: (0, o[c]))
    result = jax.ShapeDtypeStruct((depth, part * count), BF16)
    pieces = len(turned)
    return pl.pallas_call(
        functools.partial(weight_grad, pieces, factor),
        out_shape=(result, result),
        grid_spec=pltpu.PrefetchScalarGridSpec(
            num_scalar_prefetch=1,
            grid=(count,),
            in_specs=[vmem] * (pieces + len(flat)),
            out_specs=[out, out],
        ),
        compiler_params=pltpu.CompilerParams(vmem_limit_bytes=16 * MIB),
        cost_estimate=pl.CostEstimate(
            flops=2 * depth * width * count * turned[0].shape[1] * pieces,
            bytes_accessed=4 * depth * width * count,
            transcendentals=0,
        ),
        name="weight_grad",
    )(order, *turned, *flat)


def normed(values, gain):
    inverse = lax.rsqrt(jnp.mean(values * values, axis=-1, keepdims=True) + EPSILON)
    return values * inverse * gain


def visible_slots(tile_counts, image_starts, image_len, text_len):
    lengths = tile_counts * TILE_TOK
    image_upper = jnp.cumsum(lengths, axis=-1)
    image_lower = image_upper - lengths
    slot_index = jnp.arange(image_len, dtype=jnp.int32)
    text_index = jnp.arange(text_len, dtype=jnp.int32)
    inside = (
        (slot_index >= image_lower[..., None]) & (slot_index < image_upper[..., None])
    ).astype(jnp.float32)
    text_after = (text_index >= image_starts[..., None]).astype(jnp.float32)
    return jnp.einsum("...ij,...it->...jt", inside, text_after)


def attention_grads(query, grad_out, key_pre, value_rounded, visible, q_gain, k_gain):
    root_scale = 1.0 / math.sqrt(query.shape[-1])
    query_normed = normed(query.astype(jnp.float32), q_gain).astype(jnp.bfloat16)
    key_normed = normed(key_pre, k_gain).astype(jnp.bfloat16)
    scores = (
        jnp.einsum(
            "bjgd,btghd->bghjt", key_normed, query_normed, preferred_element_type=jnp.float32
        )
        * root_scale
    )
    weights = jnp.exp(scores) * visible[:, None, None]
    denominator = jnp.sum(weights, axis=3, keepdims=True)
    probability = weights / jnp.where(denominator > 0, denominator, 1.0)
    prob_rounded = probability.astype(jnp.bfloat16)
    value_grad = jnp.einsum(
        "bghjt,btghd->bjgd", prob_rounded, grad_out, preferred_element_type=jnp.float32
    ).astype(jnp.bfloat16)
    prob_grad = jnp.einsum(
        "btghd,bjgd->bghjt", grad_out, value_rounded, preferred_element_type=jnp.float32
    )
    row_delta = jnp.sum(probability * prob_grad, axis=3, keepdims=True)
    score_grad = (probability * (prob_grad - row_delta)).astype(jnp.bfloat16)
    normed_grad = (
        jnp.einsum(
            "bghjt,btghd->bjgd", score_grad, query_normed, preferred_element_type=jnp.float32
        )
        * root_scale
    )
    inverse = lax.rsqrt(jnp.mean(key_pre * key_pre, axis=-1, keepdims=True) + EPSILON)
    scaled = normed_grad * k_gain
    key_grad = inverse * scaled - key_pre * inverse**3 * jnp.mean(
        scaled * key_pre, axis=-1, keepdims=True
    )
    return (key_grad.astype(jnp.bfloat16), value_grad)


def per_device(
    queries, grad_out, features, w_key, w_value, q_gain, k_gain, tile_counts, image_starts
):
    head_dim = q_gain.shape[1]
    features_all = lax.all_gather(features, "pipe", axis=0, tiled=True)
    micro_count, image_len, quarter = features_all.shape
    slot_rows = micro_count * image_len
    flattened = features_all.reshape(slot_rows, quarter)
    weight_pair = lax.all_gather(jnp.stack([w_key[0], w_value[0]]), "dp", axis=1, tiled=True)
    key_width = weight_pair.shape[2]
    partial_kv = jnp.einsum(
        "bi,sik->bsk", flattened, weight_pair, preferred_element_type=jnp.float32
    )
    summed_kv = lax.psum_scatter(
        partial_kv.astype(jnp.bfloat16), "mp", scatter_dimension=2, tiled=True
    ).astype(jnp.float32)
    local_width = summed_kv.shape[2]
    key_heads = local_width // head_dim
    query_local = queries[0]
    text_len = query_local.shape[1]
    groups = query_local.shape[2] // local_width
    shape_q = (micro_count, text_len, key_heads, groups, head_dim)
    shape_k = (micro_count, image_len, key_heads, head_dim)
    visible = visible_slots(tile_counts[:, 0], image_starts[:, 0], image_len, text_len)
    key_grad, value_grad = attention_grads(
        query_local.reshape(shape_q),
        grad_out[0].reshape(shape_q),
        summed_kv[:, 0].reshape(shape_k),
        summed_kv[:, 1].astype(jnp.bfloat16).reshape(shape_k),
        visible,
        q_gain[0],
        k_gain[0],
    )
    local_grads = jnp.stack(
        [key_grad.reshape(slot_rows, local_width), value_grad.reshape(slot_rows, local_width)],
        axis=1,
    )
    kv_grads = lax.all_gather(local_grads, "mp", axis=2, tiled=True)
    image_grads = lax.psum_scatter(
        jnp.einsum("bsk,sik->bi", kv_grads, weight_pair, preferred_element_type=jnp.float32).astype(
            jnp.bfloat16
        ),
        "pipe",
        scatter_dimension=0,
        tiled=True,
    ).astype(jnp.float32)
    dp_count = lax.axis_size("dp")
    factor = 1.0 / (micro_count * dp_count)
    columns = lax.all_to_all(flattened, "dp", split_axis=1, concat_axis=0, tiled=True)
    every_grad = lax.all_gather(kv_grads, "dp", axis=0, tiled=True)
    columns = columns.reshape(dp_count, slot_rows, quarter // dp_count)
    every_grad = every_grad.reshape(dp_count, slot_rows, 2, key_width)
    replica_terms = jnp.einsum(
        "rbi,rbsk->risk", columns, every_grad, preferred_element_type=jnp.float32
    ).astype(jnp.bfloat16)
    replica_terms = lax.optimization_barrier(replica_terms)
    summed = jnp.sum(replica_terms.astype(jnp.float32), axis=0)
    scaled_grads = (summed * factor).astype(jnp.bfloat16)
    return (
        image_grads.reshape(1, image_len, quarter).astype(jnp.bfloat16),
        scaled_grads[:, 0][None],
        scaled_grads[:, 1][None],
    )


def solution(mesh):
    in_specs = (
        P("pipe", None, "dp", "mp"),
        P("pipe", None, "dp", "mp"),
        P("pipe", "dp", "mp"),
        P("pipe", ("mp", "dp"), None),
        P("pipe", ("mp", "dp"), None),
        P("pipe", None),
        P("pipe", None),
        P(None, "dp", None),
        P(None, "dp", None),
    )
    out_specs = (
        P("pipe", "dp", "mp"),
        P("pipe", ("mp", "dp"), None),
        P("pipe", ("mp", "dp"), None),
    )
    paired = (mesh.shape["pipe"], mesh.shape["dp"], mesh.shape["mp"]) == (4, 2, 4)
    return jax.shard_map(
        per_device_pair if paired else per_device,
        mesh=mesh,
        in_specs=in_specs,
        out_specs=out_specs,
        check_vma=False,
    )
```

```python
import functools
import math

import jax
import jax.numpy as jnp
from jax import lax
from jax.experimental import pallas as pl
from jax.experimental.pallas import tpu as pltpu
from jax.sharding import PartitionSpec as P


TILE_TOK = 16


EPSILON = 1e-05
ORDER = (0, 2, 1, 3)
SEQUENCE = (2, 3, 1, 0)
HOW = (
    (2, 0, 0, 2),
    (0, 1, 2, 1),
    (0, 0, 1, 1),
    (0, 0, 2, 3),
)
PLAN = (
    ("replica", 0, 1),
    ("mine", 1, 1),
    ("mine", 2, 1),
    ("fetch", 0, 0),
    ("theirs", 1, 1),
    ("theirs", 2, 1),
    ("early", 0, 1),
    ("project", 2, 2),
    ("mine", 3, 1),
    ("project", 0, 1),
    ("theirs", 3, 1),
    ("project", 1, 2),
    ("first", 2, 1),
    ("first", 0, 1),
    ("project", 3, 2),
    ("norm", 0, 0),
    ("first", 1, 2),
    ("second", 2, 1),
    ("second", 1, 1),
    ("first", 3, 2),
    ("second", 0, 1),
    ("attention", 2, 2),
    ("attention", 0, 2),
    ("attention", 1, 1),
    ("turn", 3, 0),
    ("turn", 0, 0),
    ("far_pass", 2, 1),
    ("second", 3, 1),
    ("far", 0, 2),
    ("turn", 2, 0),
    ("far", 1, 2),
    ("near", 0, 1),
    ("attention", 3, 1),
    ("near", 2, 1),
    ("turn", 1, 0),
    ("near_pass", 1, 1),
    ("image", 0, 2),
    ("far", 3, 2),
    ("image", 1, 2),
    ("near_pass", 3, 1),
    ("image", 2, 1),
    ("part", 1, 0),
    ("part", 0, 0),
    ("part", 2, 0),
    ("total", 3, 1),
    ("other", 3, 1),
    ("weights", 3, 0),
)


F32 = jnp.float32
BF16 = jnp.bfloat16
MIB = 1024 * 1024


def dot_nt(a, b):
    return lax.dot_general(a, b, (((1,), (1,)), ((), ())), preferred_element_type=F32)


def dot_nn(a, b):
    return lax.dot_general(a, b, (((1,), (0,)), ((), ())), preferred_element_type=F32)


def swap(values, axis, distance):
    size = lax.axis_size(axis)
    return lax.ppermute(values, axis, [(i, i ^ distance) for i in range(size)])


class Line:
    def __init__(self):
        self.last = None
        self.at = 0

    def __call__(
        self, body, outs, scalars, arrays, flops=0, scratch=(), limit=16, space=pltpu.VMEM
    ):
        vmem = pl.BlockSpec(memory_space=pltpu.VMEM)
        given = pl.BlockSpec(memory_space=space)
        smem = pl.BlockSpec(memory_space=pltpu.SMEM)
        after = [] if self.last is None else [self.last]
        inputs = len(scalars) + len(arrays)

        def kernel(*refs):
            body(*refs[:inputs], *refs[inputs + len(after) :])

        moved = sum(2 * a.size for a in arrays)
        call = pl.pallas_call(
            kernel,
            out_shape=outs,
            in_specs=[smem] * len(scalars)
            + [given] * len(arrays)
            + [pl.BlockSpec(memory_space=pl.ANY)] * len(after),
            out_specs=[vmem] * len(outs),
            scratch_shapes=list(scratch),
            cost_estimate=pl.CostEstimate(flops=flops, bytes_accessed=moved, transcendentals=0),
            compiler_params=pltpu.CompilerParams(vmem_limit_bytes=limit * MIB),
        )
        results = call(*scalars, *arrays, *after)
        self.at += 1
        self.last = results[-1]
        return results


def shape(*dims, kind=BF16):
    return jax.ShapeDtypeStruct(dims, kind)


def columns(place_ref, c, part):
    return pl.ds(pl.multiple_of(place_ref[c] * part, part), part)


def fetch(place_ref, tiles_ref, starts_ref, wk_ref, wv_ref, out_ref):
    del place_ref, tiles_ref, starts_ref, wk_ref, wv_ref
    out_ref[...] = jnp.zeros_like(out_ref)


def query_norm(q_ref, gain_ref, out_ref):
    gain = gain_ref[...]
    head_dim = gain.shape[1]
    for micro in range(q_ref.shape[0]):
        for start in range(0, q_ref.shape[2], head_dim):
            head = q_ref[micro, :, start : start + head_dim].astype(F32)
            inverse = lax.rsqrt(jnp.mean(head * head, axis=-1, keepdims=True) + EPSILON)
            out_ref[micro, :, start : start + head_dim] = (head * inverse * gain).astype(BF16)


def turn(mine_ref, theirs_ref, out_ref):
    rows = mine_ref.shape[0]
    for replica, slots_ref in enumerate((mine_ref, theirs_ref)):
        out_ref[:, replica * rows : (replica + 1) * rows] = slots_ref[...].T


def project(groups, place_ref, *refs):
    outs = refs[-len(groups) :]
    *slot_refs, wk_ref, wv_ref = refs[: -len(groups)]
    rows = slot_refs[0].shape[0]
    part = outs[0].shape[-1] // 2
    slots = jnp.concatenate([ref[...] for ref in slot_refs], axis=0)
    quarters = sorted({quarter for group in groups for _, quarter in group})
    for c in quarters:
        for at, weight in ((0, wk_ref), (part, wv_ref)):
            out = dot_nn(slots, weight[:, columns(place_ref, c, part)])
            for group, out_ref in zip(groups, outs):
                for n, (which, quarter) in enumerate(group):
                    if quarter == c:
                        term = out[which * rows : (which + 1) * rows]
                        out_ref[n, :, at : at + part] = term.astype(out_ref.dtype)


def read(refs, place):
    ref, index = place
    return refs[ref][...] if index is None else refs[ref][index]


def add_up(sums, *refs):
    outs = refs[len(refs) - len(sums) :]
    for rows, out_ref in zip(sums, outs):
        for n, pieces in enumerate(rows):
            total = read(refs, pieces[0]).astype(F32)
            for piece in pieces[1:]:
                total = total + read(refs, piece).astype(F32)
            if len(out_ref.shape) == 2:
                out_ref[...] = total.astype(BF16)
            else:
                out_ref[n] = total.astype(BF16)


def stack_up(*refs):
    *parts, out_ref = refs
    at = 0
    for ref in parts:
        if len(ref.shape) < len(out_ref.shape):
            out_ref[at] = ref[...]
            at += 1
        else:
            out_ref[at : at + ref.shape[0]] = ref[...]
            at += ref.shape[0]


def attention(relative, pieces, place_ref, tiles_ref, starts_ref, q_ref, go_ref, gain_ref, *refs):
    out_ref = refs[-1]
    micro = place_ref[len(ORDER) + relative]
    gain = gain_ref[...]
    head_dim = gain.shape[1]
    summed = read(refs, pieces[0]).astype(F32)
    for piece in pieces[1:]:
        summed = summed + read(refs, piece).astype(F32)
    image_len, width = summed.shape
    local_width = width // 2
    key_heads = local_width // head_dim
    text_len = q_ref.shape[1]
    groups = q_ref.shape[2] // local_width
    root_scale = 1.0 / math.sqrt(head_dim)
    slot = lax.broadcasted_iota(jnp.int32, (image_len, text_len), 0)
    text = lax.broadcasted_iota(jnp.int32, (image_len, text_len), 1)
    seen = jnp.zeros((image_len, text_len), F32)
    lower = jnp.int32(0)
    for image in range(tiles_ref.shape[2]):
        upper = lower + tiles_ref[micro, 0, image] * TILE_TOK
        inside = (slot >= lower) & (slot < upper) & (text >= starts_ref[micro, 0, image])
        seen = jnp.where(inside, 1.0, seen)
        lower = upper
    seen = jnp.concatenate([seen] * groups, axis=1)
    for g in range(key_heads):
        key_pre = summed[:, g * head_dim : (g + 1) * head_dim]
        value = summed[:, local_width + g * head_dim : local_width + (g + 1) * head_dim]
        value = value.astype(BF16)
        inverse = lax.rsqrt(jnp.mean(key_pre * key_pre, axis=-1, keepdims=True) + EPSILON)
        key = (key_pre * inverse * gain).astype(BF16)
        heads = [(g * groups + h) * head_dim for h in range(groups)]
        query = jnp.concatenate([q_ref[micro, :, h : h + head_dim] for h in heads], axis=0)
        grad = jnp.concatenate([go_ref[micro, :, h : h + head_dim] for h in heads], axis=0)
        weights = jnp.exp(dot_nt(key, query) * root_scale) * seen
        total = jnp.sum(weights, axis=0, keepdims=True)
        probability = weights * (1.0 / jnp.where(total > 0, total, 1.0))
        value_grad = dot_nn(probability.astype(BF16), grad)
        prob_grad = dot_nt(value, grad)
        delta = jnp.sum(probability * prob_grad, axis=0, keepdims=True)
        score_grad = (probability * (prob_grad - delta)).astype(BF16)
        scaled = dot_nn(score_grad, query) * root_scale * gain
        key_grad = inverse * scaled - key_pre * inverse**3 * jnp.mean(
            scaled * key_pre, axis=-1, keepdims=True
        )
        out_ref[:, g * head_dim : (g + 1) * head_dim] = key_grad.astype(BF16)
        at = local_width + g * head_dim
        out_ref[:, at : at + head_dim] = value_grad.astype(BF16)


def grad_terms(place_ref, grads, wk_ref, wv_ref, begin=0, parts=1):
    part = grads[0][0].shape[1] // 2
    depth = wk_ref.shape[0] // parts
    tile = min(depth, 256)
    count = len(grads[0])
    rows = grads[0][0].shape[0]
    every = jnp.concatenate([jnp.concatenate(list(g), axis=1) for g in grads], axis=0)
    for start in range(0, depth, tile):
        row = begin * depth + start
        weights = jnp.concatenate(
            [
                weight[row : row + tile, columns(place_ref, c, part)]
                for c in range(count)
                for weight in (wk_ref, wv_ref)
            ],
            axis=1,
        )
        out = dot_nt(every, weights)
        yield start, tile, out[:rows], out[rows:]


def feature_grad(own, other, packs, place_ref, *refs):
    inputs = 1 + max(ref for ref, _ in own + other)
    wk_ref, wv_ref, *outs = refs[inputs:]
    if packs:
        for out_ref, places in zip(outs[:2], (own, other)):
            for c, place in enumerate(places):
                out_ref[c] = read(refs, place)
        outs = outs[2:]
    theirs_ref, mine_ref = outs if len(outs) == 2 else (outs[0].at[0], outs[0].at[1])
    grads = [[read(refs, place) for place in places] for places in (own, other)]
    for start, tile, mine, theirs in grad_terms(place_ref, grads, wk_ref, wv_ref):
        theirs_ref[:, start : start + tile] = theirs.astype(BF16)
        mine_ref[:, start : start + tile] = mine.astype(BF16)


def feature_total(own, other, packs, begin, place_ref, *refs):
    inputs = 1 + max(ref for ref, _ in own + other)
    wk_ref, wv_ref, *rest = refs[inputs:]
    *terms, mine_ref, theirs_ref = rest
    if packs:
        *terms, own_ref, other_ref = terms
        for out_ref, places in ((own_ref, own), (other_ref, other)):
            for c, place in enumerate(places):
                out_ref[c] = read(refs, place)
    grads = [[read(refs, place) for place in places] for places in (own, other)]
    width = mine_ref.shape[1]
    for start, tile, mine, theirs in grad_terms(place_ref, grads, wk_ref, wv_ref, begin, 2):
        mine_ref[:, start : start + tile] = mine
        at = begin * width + start
        for term in terms:
            if len(term.shape) == 3:
                term = term.at[0]
            theirs = theirs + term[:, at : at + tile].astype(F32)
        theirs_ref[:, start : start + tile] = theirs.astype(BF16)


def weight_part(turned_ref, own_ref, other_ref, *refs):
    *before, out_ref = refs
    slots = turned_ref[...]
    for c in range(own_ref.shape[0]):
        every = jnp.concatenate([own_ref[c], other_ref[c]], axis=0)
        term = dot_nn(slots, every)
        out_ref[c] = before[0][c] + term if before else term


def weight_grad(factor, place_ref, sum_ref, turned_ref, own_ref, other_ref, _, key_ref, value_ref):
    part = key_ref.shape[1]
    step = pl.program_id(0)
    every = jnp.concatenate([own_ref[step], other_ref[step]], axis=0)
    total = (sum_ref[step] + dot_nn(turned_ref[...], every)) * factor
    key_ref[...] = total[:, :part].astype(BF16)
    value_ref[...] = total[:, part:].astype(BF16)


def join_outputs(place_ref, *refs):
    *terms, out_ref = refs
    theirs, mines, rest = terms[:2], terms[2:4], terms[4:]
    width = mines[0].shape[1]
    replica = place_ref[place_ref.shape[0] - 1]
    for n in range(2):
        mine = mines[n][...]
        for term in rest:
            if len(term.shape) == 3:
                term = term.at[1]
            mine = mine + term[:, n * width : (n + 1) * width].astype(F32)
        mine = mine.astype(BF16)
        for at in range(2):

            @pl.when(replica == at)
            def _():
                start = 2 * at * width + n * width
                out_ref[:, start : start + width] = mine
                start = 2 * (1 - at) * width + n * width
                out_ref[:, start : start + width] = theirs[n][...]


def per_device_pair(*args):
    return pair_program(*args)


def pair_program(
    queries, grad_out, features, w_key, w_value, q_gain, k_gain, tile_counts, image_starts
):
    own_pipe = lax.axis_index("pipe")
    own_dp = lax.axis_index("dp")
    own_mp = lax.axis_index("mp")
    micro_count = queries.shape[1]
    place = jnp.stack(
        [own_mp ^ c for c in ORDER] + [own_pipe ^ j for j in range(micro_count)] + [own_dp]
    ).astype(jnp.int32)
    w_key = w_key[0]
    w_value = w_value[0]
    half, key_width = w_key.shape
    local = features[0]
    image_len = local.shape[0]
    count = len(ORDER)
    width = 2 * key_width // count
    dense = 4 * 2 * image_len * half * key_width

    mine = lax.dynamic_slice(local, (0, own_dp * half), (image_len, half))
    theirs = lax.dynamic_slice(local, (0, (1 - own_dp) * half), (image_len, half))
    features = {"mine": {0: mine}, "theirs": {}}

    line = Line()
    near, far = ("mp", 1), ("mp", 2)
    cross = ("dp", 1)
    keep, got, sums, grad, heads, image, rest, turned, packed = ({} for _ in range(9))
    own_halves, other_halves = [], []
    query = outputs = weight_sum = None
    block = shape(image_len, width)
    two = shape(2, image_len, width)
    four = shape(count, image_len, width)
    wide = shape(count, image_len, width, kind=F32)
    halved = shape(2, image_len, width, kind=F32)

    def send(values, link):
        return swap(values, *link)

    for stage, i, _ in PLAN:
        j = SEQUENCE[i]
        late, early, late_split, early_split = HOW[i]
        if stage == "replica":
            features["theirs"][0] = send(theirs, cross)
        elif stage in features:
            held = features[stage]
            held[i] = send(held[0 if i < 3 else 2], ("pipe", 1 if i == 3 else i))
        elif stage == "fetch":
            line(
                fetch,
                [shape(8, 128, kind=F32)],
                [place, tile_counts, image_starts],
                [w_key, w_value],
            )
        elif stage == "norm":
            (query,) = line(query_norm, [shape(*queries.shape[1:])], [], [queries[0], q_gain])
        elif stage == "turn":
            parts = [features["mine"][j], features["theirs"][j]]
            (turned[j],) = line(turn, [shape(half, 2 * image_len)], [], parts)
        elif stage == "early" or (stage == "project" and late == 2):
            own_slots = stage == "early"
            kept, out = line(
                functools.partial(project, (((0, 0), (0, 1)), ((0, 2), (0, 3)))),
                [halved, two],
                [place],
                [features["mine" if own_slots else "theirs"][j], w_key, w_value],
                dense // 2,
            )
            received = send(out, near)
            keep.setdefault(j, {})[0 if own_slots else 1] = kept
            got.setdefault(j, {})[0 if own_slots else 1] = received
        elif stage == "project":
            parts = [features["mine"][j], features["theirs"][j], w_key, w_value]
            if late:
                groups = (
                    ((0, 0), (0, 1)),
                    ((1, 0), (1, 1)),
                    ((0, 2), (0, 3), (1, 2), (1, 3)),
                )
                kept, other_kept, out = line(
                    functools.partial(project, groups), [halved, halved, four], [place], parts, dense
                )
                keep[j] = {0: kept, 1: other_kept}
                got[j] = send(out, near)
            elif late_split:
                groups = (
                    tuple((0, c) for c in range(count)),
                    ((1, 2), (1, 3)),
                    ((1, 0), (1, 1)),
                )
                keep[j], out, later = line(
                    functools.partial(project, groups), [wide, two, two], [place], parts, dense
                )
                got[j] = {1: send(out, cross)}
                got[j][0] = send(later, cross)
            else:
                groups = (
                    tuple((0, c) for c in range(count)),
                    tuple((1, c) for c in range(count)),
                )
                keep[j], out = line(
                    functools.partial(project, groups), [wide, four], [place], parts, dense
                )
                got[j] = send(out, cross)
        elif stage == "first" and late:
            if late == 2:
                parts = [keep[j][0], keep[j][1], got[j][0], got[j][1]]
                rows = [((0, 1), (2, 1)), ((1, 1), (3, 1))]
            else:
                parts = [keep[j][0], keep[j][1], got[j]]
                rows = [((0, 1), (2, 1)), ((1, 1), (2, 3))]
            (out,) = line(functools.partial(add_up, [rows]), [two], [], parts)
            sums[j] = [send(out, far)]
        elif stage == "second" and late:
            if late == 2:
                parts = [keep[j][1], got[j][1], sums[j][0]]
                rows = [((0, 0), (1, 0), (2, 1))]
            else:
                parts = [keep[j][1], got[j], sums[j][0]]
                rows = [((0, 0), (1, 2), (2, 1))]
            (out,) = line(functools.partial(add_up, [rows]), [block], [], parts)
            own_parts = [keep[j][0], got[j][0] if late == 2 else got[j], sums[j][0]]
            sums[j] = (own_parts + [send(out, cross)], (0, 0, 0, None))
        elif stage == "first":
            split = late_split > 0
            lead = got[j][1] if split else got[j]
            at = 0 if split else 2
            rows = [[((0, 2 + n), (1, at + n))] for n in range(2)]
            if late_split == 2:
                out, later = line(
                    functools.partial(add_up, [rows[1], rows[0]]), [block, block], [], [keep[j], lead]
                )
                sums[j] = [send(out, near)]
                sums[j].append(send(later, near))
            else:
                (out,) = line(
                    functools.partial(add_up, [rows[0] + rows[1]]), [two], [], [keep[j], lead]
                )
                sums[j] = [send(out, near)]
        elif stage == "second":
            lead = got[j][0] if late_split else got[j]
            index = None if late_split == 2 else 1
            (out,) = line(
                functools.partial(add_up, [[((0, 1), (1, 1), (2, index))]]),
                [block],
                [],
                [keep[j], lead, sums[j][0]],
            )
            own_parts = [keep[j], lead, sums[j][-1], send(out, far)]
            sums[j] = (own_parts, (0, 0, None if late_split == 2 else 0, None))
        elif stage == "attention":
            parts, indices = sums[j]
            (grad[j],) = line(
                functools.partial(attention, j, tuple(enumerate(indices))),
                [block],
                [place, tile_counts, image_starts],
                [query, grad_out[0], k_gain, *parts],
                dense // 2,
            )
            heads[j] = [grad[j], send(grad[j], cross if early else far)]
            if not early and early_split in (1, 2):
                heads[j].append(send(grad[j], near))
        elif stage == "far_pass":
            heads[j].append(send(heads[j][1], near))
        elif stage == "far":
            (both,) = line(stack_up, [two], [], heads[j][:2])
            if early:
                heads[j] = [both, send(both, far)]
                if early_split:
                    heads[j].append(send(both, near))
            elif early_split == 2:
                received = send(heads[j][1], near)
                heads[j] = [both, heads[j][2], received, send(both, cross)]
            else:
                heads[j] = [both, send(both, near)]
                if early_split == 3:
                    heads[j].append(send(both, cross))
        elif stage == "near_pass":
            heads[j].append(send(heads[j][1], near if early else cross))
        elif stage == "near":
            if early:
                parts, result = heads[j], shape(2, 2, image_len, width)
            elif early_split == 2:
                parts, result = heads[j][1:3], two
            else:
                parts, result = heads[j], four
            (out,) = line(stack_up, [result], [], parts)
            received = send(out, near if early else cross)
            if not early and early_split == 2:
                heads[j] = [heads[j][0], out, heads[j][3], received]
            else:
                heads[j] = [out, received]
        elif stage == "part":
            before = [] if weight_sum is None else [weight_sum]
            (weight_sum,) = line(
                weight_part,
                [shape(count, half, width, kind=F32)],
                [],
                [turned[j], *packed[j], *before],
                dense,
            )
        elif stage in ("image", "total", "other"):
            if early and early_split:
                own, other = (tuple((n, r) for n in range(count)) for r in range(2))
            elif early:
                own, other = (
                    tuple((n, (c, r)) for n in range(2) for c in range(2)) for r in range(2)
                )
            elif early_split >= 2:
                own, other = (
                    tuple((2 * r + n, c) for n in range(2) for c in range(2)) for r in range(2)
                )
            else:
                own, other = (tuple((r, c) for c in range(count)) for r in range(2))
            packs = early or early_split >= 2
            where = (own, other, packs)
            part = shape(image_len, half)
            outs = [four, four] if packs else []
            parts = [*heads[j], w_key, w_value]
            if stage == "image":
                whole = [shape(2, image_len, half)] if j == 1 else [part, part]
                results = line(
                    functools.partial(feature_grad, *where), outs + whole, [place], parts, dense
                )
                packed[j] = results[: len(outs)]
                sends = [send(out, ("pipe", j)) for out in results[len(outs) :]]
                image[j], rest[j] = sends[0], sends[-1]
            else:
                begin = int(stage == "other")
                packs = packs and not begin
                *copies, mine_part, theirs_part = line(
                    functools.partial(feature_total, own, other, packs, begin),
                    (outs if packs else [])
                    + [shape(image_len, half // 2, kind=F32), shape(image_len, half // 2)],
                    [place],
                    parts + list(image.values()),
                    dense // 2,
                )
                own_halves.append(mine_part)
                other_halves.append(send(theirs_part, cross))
                if packs:
                    packed[j] = copies
            if not early and early_split < 2:
                packed[j] = heads[j]
        elif stage == "weights":
            factor = 1.0 / (micro_count * 2)
            outputs = weight_outputs(
                place, weight_sum, turned[j], packed[j], factor, line.last
            )
            line.last = None
    (image_grads,) = line(
        join_outputs,
        [shape(image_len, 2 * half)],
        [place],
        other_halves + own_halves + list(rest.values()),
    )
    return image_grads[None], outputs[0][None], outputs[1][None]


def weight_outputs(place, weight_sum, turned, grads, factor, after):
    count, depth, width = weight_sum.shape
    part = width // 2
    vmem = pl.BlockSpec(memory_space=pltpu.VMEM)
    out = pl.BlockSpec((depth, part), lambda c, o: (0, o[c]))
    result = jax.ShapeDtypeStruct((depth, part * count), BF16)
    return pl.pallas_call(
        functools.partial(weight_grad, factor),
        out_shape=(result, result),
        grid_spec=pltpu.PrefetchScalarGridSpec(
            num_scalar_prefetch=1,
            grid=(count,),
            in_specs=[vmem] * 4 + [pl.BlockSpec(memory_space=pl.ANY)],
            out_specs=[out, out],
        ),
        compiler_params=pltpu.CompilerParams(vmem_limit_bytes=16 * MIB),
        cost_estimate=pl.CostEstimate(
            flops=2 * depth * width * count * turned.shape[1],
            bytes_accessed=4 * depth * width * count,
            transcendentals=0,
        ),
        name="weight_grad",
    )(place, weight_sum, turned, *grads, after)


def normed(values, gain):
    inverse = lax.rsqrt(jnp.mean(values * values, axis=-1, keepdims=True) + EPSILON)
    return values * inverse * gain


def visible_slots(tile_counts, image_starts, image_len, text_len):
    lengths = tile_counts * TILE_TOK
    image_upper = jnp.cumsum(lengths, axis=-1)
    image_lower = image_upper - lengths
    slot_index = jnp.arange(image_len, dtype=jnp.int32)
    text_index = jnp.arange(text_len, dtype=jnp.int32)
    inside = (
        (slot_index >= image_lower[..., None]) & (slot_index < image_upper[..., None])
    ).astype(jnp.float32)
    text_after = (text_index >= image_starts[..., None]).astype(jnp.float32)
    return jnp.einsum("...ij,...it->...jt", inside, text_after)


def attention_grads(query, grad_out, key_pre, value_rounded, visible, q_gain, k_gain):
    root_scale = 1.0 / math.sqrt(query.shape[-1])
    query_normed = normed(query.astype(jnp.float32), q_gain).astype(jnp.bfloat16)
    key_normed = normed(key_pre, k_gain).astype(jnp.bfloat16)
    scores = (
        jnp.einsum(
            "bjgd,btghd->bghjt", key_normed, query_normed, preferred_element_type=jnp.float32
        )
        * root_scale
    )
    weights = jnp.exp(scores) * visible[:, None, None]
    denominator = jnp.sum(weights, axis=3, keepdims=True)
    probability = weights / jnp.where(denominator > 0, denominator, 1.0)
    prob_rounded = probability.astype(jnp.bfloat16)
    value_grad = jnp.einsum(
        "bghjt,btghd->bjgd", prob_rounded, grad_out, preferred_element_type=jnp.float32
    ).astype(jnp.bfloat16)
    prob_grad = jnp.einsum(
        "btghd,bjgd->bghjt", grad_out, value_rounded, preferred_element_type=jnp.float32
    )
    row_delta = jnp.sum(probability * prob_grad, axis=3, keepdims=True)
    score_grad = (probability * (prob_grad - row_delta)).astype(jnp.bfloat16)
    normed_grad = (
        jnp.einsum(
            "bghjt,btghd->bjgd", score_grad, query_normed, preferred_element_type=jnp.float32
        )
        * root_scale
    )
    inverse = lax.rsqrt(jnp.mean(key_pre * key_pre, axis=-1, keepdims=True) + EPSILON)
    scaled = normed_grad * k_gain
    key_grad = inverse * scaled - key_pre * inverse**3 * jnp.mean(
        scaled * key_pre, axis=-1, keepdims=True
    )
    return (key_grad.astype(jnp.bfloat16), value_grad)


def per_device(
    queries, grad_out, features, w_key, w_value, q_gain, k_gain, tile_counts, image_starts
):
    head_dim = q_gain.shape[1]
    features_all = lax.all_gather(features, "pipe", axis=0, tiled=True)
    micro_count, image_len, quarter = features_all.shape
    slot_rows = micro_count * image_len
    flattened = features_all.reshape(slot_rows, quarter)
    weight_pair = lax.all_gather(jnp.stack([w_key[0], w_value[0]]), "dp", axis=1, tiled=True)
    key_width = weight_pair.shape[2]
    partial_kv = jnp.einsum(
        "bi,sik->bsk", flattened, weight_pair, preferred_element_type=jnp.float32
    )
    summed_kv = lax.psum_scatter(
        partial_kv.astype(jnp.bfloat16), "mp", scatter_dimension=2, tiled=True
    ).astype(jnp.float32)
    local_width = summed_kv.shape[2]
    key_heads = local_width // head_dim
    query_local = queries[0]
    text_len = query_local.shape[1]
    groups = query_local.shape[2] // local_width
    shape_q = (micro_count, text_len, key_heads, groups, head_dim)
    shape_k = (micro_count, image_len, key_heads, head_dim)
    visible = visible_slots(tile_counts[:, 0], image_starts[:, 0], image_len, text_len)
    key_grad, value_grad = attention_grads(
        query_local.reshape(shape_q),
        grad_out[0].reshape(shape_q),
        summed_kv[:, 0].reshape(shape_k),
        summed_kv[:, 1].astype(jnp.bfloat16).reshape(shape_k),
        visible,
        q_gain[0],
        k_gain[0],
    )
    local_grads = jnp.stack(
        [key_grad.reshape(slot_rows, local_width), value_grad.reshape(slot_rows, local_width)],
        axis=1,
    )
    kv_grads = lax.all_gather(local_grads, "mp", axis=2, tiled=True)
    image_grads = lax.psum_scatter(
        jnp.einsum("bsk,sik->bi", kv_grads, weight_pair, preferred_element_type=jnp.float32).astype(
            jnp.bfloat16
        ),
        "pipe",
        scatter_dimension=0,
        tiled=True,
    ).astype(jnp.float32)
    dp_count = lax.axis_size("dp")
    factor = 1.0 / (micro_count * dp_count)
    columns = lax.all_to_all(flattened, "dp", split_axis=1, concat_axis=0, tiled=True)
    every_grad = lax.all_gather(kv_grads, "dp", axis=0, tiled=True)
    columns = columns.reshape(dp_count, slot_rows, quarter // dp_count)
    every_grad = every_grad.reshape(dp_count, slot_rows, 2, key_width)
    replica_terms = jnp.einsum(
        "rbi,rbsk->risk", columns, every_grad, preferred_element_type=jnp.float32
    ).astype(jnp.bfloat16)
    replica_terms = lax.optimization_barrier(replica_terms)
    summed = jnp.sum(replica_terms.astype(jnp.float32), axis=0)
    scaled_grads = (summed * factor).astype(jnp.bfloat16)
    return (
        image_grads.reshape(1, image_len, quarter).astype(jnp.bfloat16),
        scaled_grads[:, 0][None],
        scaled_grads[:, 1][None],
    )


def solution(mesh):
    in_specs = (
        P("pipe", None, "dp", "mp"),
        P("pipe", None, "dp", "mp"),
        P("pipe", "dp", "mp"),
        P("pipe", ("mp", "dp"), None),
        P("pipe", ("mp", "dp"), None),
        P("pipe", None),
        P("pipe", None),
        P(None, "dp", None),
        P(None, "dp", None),
    )
    out_specs = (
        P("pipe", "dp", "mp"),
        P("pipe", ("mp", "dp"), None),
        P("pipe", ("mp", "dp"), None),
    )
    paired = (mesh.shape["pipe"], mesh.shape["dp"], mesh.shape["mp"]) == (4, 2, 4)
    return jax.shard_map(
        per_device_pair if paired else per_device,
        mesh=mesh,
        in_specs=in_specs,
        out_specs=out_specs,
        check_vma=False,
    )
```
